256 devices in a mesh: depth: 8 (over y, core), illum: 32 (over x, z).
Axes of the slice: x: 4, y: 4, z: 8, core: 2. Of those that a mesh axis runs over, the one named last changes fastest.
Arguments:
- fields: bfloat16 [24, 64, 2, 256, 256], P('depth', 'illum'), may hold values from -3.5 to 3.5
- screen_real: float32 [24, 256, 256], P('depth'), may hold values from 0.85 to 1.1
- screen_imag: float32 [24, 256, 256], P('depth'), may hold values from -0.3 to 0.3
- measured: float32 [64, 256, 256], P('illum'), may hold values from 0.2 to 2.5
- angles: int32 [64], P('illum'), may hold values from 0 to 255
Outputs:
- gradient: float32 [24, 2, 256, 256], P('depth', None, 'illum')
The draws below stay inside these ranges and needn't reach their ends.
All inputs are finite; a program needn't handle non-finite values.
Results may differ from the reference program's by a relative error of at most 0.0003.
Values sent between devices are 32-bit elements; how exact they have to be, the bound alone decides.
No kernel may reach another device: no remote copies, remote signals or barrier semaphores. Data moves between devices by JAX's collectives and lax.ppermute only.
A program may use at most 64 MiB of HBM per device.

```python
import jax
import jax.numpy as jnp
from jax import lax

LAT = 256
ANGLES = 256
SLICES = 24
ILLUMS = 64


def with_ends(values, stream_key, least, largest):
    longest = values.shape.index(max(values.shape))
    spots = []
    for shift in (0, 1):
        where = [jax.random.randint(jax.random.fold_in(stream_key, axis), (), 0, length) for axis, length in enumerate(values.shape)]
        where[longest] = (where[longest] + shift) % values.shape[longest]
        spots.append(tuple(where))
    return values.at[spots[0]].set(least).at[spots[1]].set(largest)


def level_of(key, shape, shards, least, top_value):
    factor_of, own = 1.0, jax.random.fold_in(key, 6)
    for position, shards_of in shards:
        heights = jnp.exp(jax.random.uniform(jax.random.fold_in(own, position), (shards_of,), jnp.float32, least / len(shards), top_value / len(shards)))
        factor_of = factor_of * jnp.repeat(heights, shape[position] // shards_of).reshape([-1 if axis == position else 1 for axis in range(len(shape))])
    return factor_of


def bell_draw(key, shape, width, reach, cuts=(), held_as=jnp.bfloat16):
    gain = level_of(key, shape, cuts, -0.22, 0.18) if cuts else 1.0
    entries = jax.random.normal(key, shape, jnp.float32) * width * gain
    return jnp.minimum(jnp.maximum(entries, -reach), reach).astype(held_as)


def setup_inputs(seed: int = 0) -> dict:
    streams_of = jax.random.split(jax.random.key(seed), 6)
    return {
        "fields": bell_draw(streams_of[0], (SLICES, ILLUMS, 2, LAT, LAT), 0.7, 3.5, ((0, 8), (1, 32))),
        "screen_real": jnp.clip(0.85 + 0.25 * jax.random.uniform(streams_of[1], (SLICES, LAT, LAT), jnp.float32) ** level_of(streams_of[1], (SLICES, LAT, LAT), ((0, 8),), -0.2, 0.2), 0.85, 1.1),
        "screen_imag": jnp.clip(jax.random.uniform(streams_of[2], (SLICES, LAT, LAT), jnp.float32, -0.3, 0.3) * level_of(streams_of[2], (SLICES, LAT, LAT), ((0, 8),), -0.4, 0.0), -0.3, 0.3),
        "measured": jnp.clip(0.2 + 2.3 * jax.random.uniform(streams_of[3], (ILLUMS, LAT, LAT), jnp.float32) ** level_of(streams_of[3], (ILLUMS, LAT, LAT), ((0, 32),), -0.2, 0.2), 0.2, 2.5),
        "angles": with_ends(jax.random.randint(streams_of[4], (ILLUMS,), 0, ANGLES), jax.random.fold_in(streams_of[4], 1), 0, ANGLES - 1).astype(jnp.int32),
    }


def kernel(extent):
    counter = jnp.arange(extent, dtype=jnp.int32)
    frequency = jnp.where(counter < extent // 2, counter, counter - extent)
    square = (frequency[:, None] * frequency[:, None] + frequency[None, :] * frequency[None, :]) % 1024
    kernel_phase = (2.0 * jnp.pi / 1024.0) * square.astype(jnp.float32)
    return jnp.cos(kernel_phase) - 1j * jnp.sin(kernel_phase)


def tilt(angle_index, extent):
    counter = jnp.arange(extent, dtype=jnp.int32)
    shift_x = angle_index % 16 - 8
    shift_y = angle_index // 16 - 8
    phase_int = (shift_x * counter[:, None] + shift_y * counter[None, :]) % extent
    phase_angle = (2.0 * jnp.pi / extent) * phase_int.astype(jnp.float32)
    return jnp.cos(phase_angle) + 1j * jnp.sin(phase_angle)


def reference(fields, screen_real, screen_imag, measured, angles):
    transfer = kernel(LAT)
    screens = screen_real + 1j * screen_imag
    factor = float(ILLUMS) ** -0.5

    def propagate(value, multiplier):
        return jnp.fft.ifft2(jnp.fft.fft2(value) * multiplier)

    def accumulate(index, gradient):
        stored = lax.dynamic_index_in_dim(fields, index, 1, keepdims=False).astype(jnp.float32)
        tilt_now = tilt(angles[index], LAT)
        psi_all = tilt_now[None] * (stored[:, 0] + 1j * stored[:, 1])
        leaving = propagate(screens[-1] * psi_all[-1], transfer)
        intensity = jnp.real(leaving) ** 2 + jnp.imag(leaving) ** 2
        cotangent = 2.0 * (intensity - measured[index]) * leaving

        def backward(carried, items):
            screen_now, field_now = items
            arriving = propagate(carried, jnp.conj(transfer))
            return jnp.conj(screen_now) * arriving, jnp.conj(field_now) * arriving

        _, terms = lax.scan(backward, cotangent, (screens, psi_all), reverse=True)
        return gradient + factor * jnp.stack([jnp.real(terms), jnp.imag(terms)], axis=1)

    return lax.fori_loop(0, ILLUMS, accumulate, jnp.zeros((SLICES, 2, LAT, LAT), jnp.float32))
```

```python
import functools

import jax
import jax.numpy as jnp
import ml_dtypes
import numpy as np
from jax import lax
from jax.experimental import pallas as pl
from jax.experimental.pallas import tpu as pltpu
from jax.sharding import PartitionSpec as P

BF16 = jnp.bfloat16
F32 = jnp.float32
VMEM = pl.BlockSpec(memory_space=pltpu.VMEM)
SMEM = pl.BlockSpec(memory_space=pltpu.SMEM)


def operator_matrices(extent):
    counter = np.arange(extent)
    frequency = np.where(counter < extent // 2, counter, counter - extent)
    factor = np.exp(-2j * np.pi * ((frequency * frequency) % 1024) / 1024)
    table = np.exp(-2j * np.pi * ((counter[:, None] * counter[None, :]) % extent) / extent)
    operator = (np.conj(table) * factor[None, :]) @ table / extent
    operator = 0.5 * (operator + operator.T)
    terms = []
    for matrix in (operator.real, operator.imag - operator.real, operator.real + operator.imag):
        high = matrix.astype(np.float32).astype(ml_dtypes.bfloat16)
        low = (matrix - high.astype(np.float64)).astype(np.float32).astype(ml_dtypes.bfloat16)
        terms.append(np.stack([high, low]))
    return np.stack(terms)


def dot(left, right):
    return jnp.dot(left, right, preferred_element_type=F32)


def split(value):
    high = value.astype(BF16)
    return high, (value - high.astype(F32)).astype(BF16)


def from_right(value, matrices, which):
    high, low = split(value)
    w_high, w_low = matrices[which, 0], matrices[which, 1]
    return dot(
        jnp.concatenate([high, low, high], axis=1), jnp.concatenate([w_high, w_high, w_low], axis=0)
    )


def from_left(value, matrices, which):
    high, low = split(value)
    w_high, w_low = matrices[which, 0], matrices[which, 1]
    return dot(
        jnp.concatenate([w_high, w_high, w_low], axis=1), jnp.concatenate([high, low, high], axis=0)
    )


def adjoint(real, imag, matrices):
    both = from_right(real + imag, matrices, 0)
    mid_real = both + from_right(imag, matrices, 1)
    mid_imag = both - from_right(real, matrices, 2)
    both = from_left(mid_real + mid_imag, matrices, 0)
    return both + from_left(mid_imag, matrices, 1), both - from_left(mid_real, matrices, 2)


def exit_body(psi, screen_real, screen_imag, measured, matrices, out):
    last = psi.shape[0] - 1
    s_real, s_imag = screen_real[last], screen_imag[last]
    f_real, f_imag = psi[last, 0], psi[last, 1]
    real, imag = adjoint(
        s_real * f_real - s_imag * f_imag, -(s_real * f_imag + s_imag * f_real), matrices
    )
    weight = 2.0 * (real * real + imag * imag - measured[...])
    out[0] = weight * real
    out[1] = -(weight * imag)


def section_body(scale, active, chi, psi, screen_real, screen_imag, matrices, grad_in, out, grad):
    count = psi.shape[0]
    on = active[0] == 1

    @pl.when(on)
    def _():
        out[...] = chi[...]

        def step(index, carry):
            slab = count - 1 - index
            real, imag = adjoint(out[0], out[1], matrices)
            p_real, p_imag = psi[slab, 0], psi[slab, 1]
            grad[slab, 0] = grad_in[slab, 0] + scale * (p_real * real + p_imag * imag)
            grad[slab, 1] = grad_in[slab, 1] + scale * (p_real * imag - p_imag * real)
            s_real, s_imag = screen_real[slab], screen_imag[slab]
            out[0] = s_real * real + s_imag * imag
            out[1] = s_real * imag - s_imag * real
            return carry

        lax.fori_loop(0, count, step, 0)

    @pl.when(jnp.logical_not(on))
    def _():
        grad[...] = grad_in[...]


def on_device(fields, screen_real, screen_imag, measured, angles, *, columns):
    slabs, lights, _, extent, _ = fields.shape
    segments = lax.axis_size("depth")
    position = lax.axis_index("depth")
    groups = lax.axis_size("illum")
    matrices = jnp.asarray(operator_matrices(extent))
    counter = jnp.arange(extent, dtype=jnp.int32)

    def ramp(shift):
        angle = 2.0 * jnp.pi / extent * ((shift[:, None] * counter) % extent).astype(F32)
        return jnp.cos(angle), jnp.sin(angle)

    x_cos, x_sin = ramp(angles % 16 - 8)
    y_cos, y_sin = ramp(angles // 16 - 8)
    fields = fields.astype(F32)

    def tilted(light):
        c_x, s_x = x_cos[light][:, None], x_sin[light][:, None]
        c_y, s_y = y_cos[light][None, :], y_sin[light][None, :]
        cos, sin = c_x * c_y - s_x * s_y, s_x * c_y + c_x * s_y
        real, imag = fields[:, light, 0], fields[:, light, 1]
        return jnp.stack([cos * real - sin * imag, cos * imag + sin * real], axis=1)

    psi = [tilted(light) for light in range(lights)]
    field_shape = jax.ShapeDtypeStruct((2, extent, extent), F32)
    grad_shape = jax.ShapeDtypeStruct((slabs, 2, extent, extent), F32)
    work = 18 * 2 * extent**3
    params = pltpu.CompilerParams(vmem_limit_bytes=24 << 20)
    exit_call = pl.pallas_call(
        exit_body,
        out_shape=field_shape,
        in_specs=[VMEM] * 5,
        out_specs=VMEM,
        compiler_params=params,
        cost_estimate=pl.CostEstimate(flops=work, bytes_accessed=1 << 20, transcendentals=0),
        name="exit",
    )
    section_call = pl.pallas_call(
        functools.partial(section_body, float(lights * groups) ** -0.5),
        out_shape=[field_shape, grad_shape],
        in_specs=[SMEM] + [VMEM] * 6,
        out_specs=[VMEM, VMEM],
        input_output_aliases={6: 1},
        compiler_params=params,
        cost_estimate=pl.CostEstimate(
            flops=slabs * work, bytes_accessed=1 << 20, transcendentals=0
        ),
        name="section",
    )
    state = [
        exit_call(psi[light], screen_real, screen_imag, measured[light], matrices)
        for light in range(lights)
    ]
    grad = jnp.zeros(grad_shape.shape, F32)
    for turn in range(segments):
        source = segments - 1 - turn
        active = (position == source).astype(jnp.int32)[None]
        for light in range(lights):
            left, grad = section_call(
                active, state[light], psi[light], screen_real, screen_imag, matrices, grad
            )
            if source > 0:
                state[light] = lax.ppermute(left, "depth", [(source, source - 1)])

    rows = extent // groups
    inner = groups // columns
    here = lax.axis_index("illum")
    here_x, here_z = here // inner, here % inner

    def block(value, start, size):
        return lax.dynamic_slice_in_dim(value, start, size, axis=2)

    wide = rows * inner
    total = block(grad, here_x * wide, wide)
    for step in range(1, columns):
        pairs = [
            (x * inner + z, (x + step) % columns * inner + z)
            for x in range(columns)
            for z in range(inner)
        ]
        sent = block(grad, (here_x + step) % columns * wide, wide)
        total = total + lax.ppermute(sent, "illum", pairs)
    result = block(total, here_z * rows, rows)
    for step in range(1, inner):
        pairs = [
            (x * inner + z, x * inner + (z + step) % inner)
            for x in range(columns)
            for z in range(inner)
        ]
        sent = block(total, (here_z + step) % inner * rows, rows)
        result = result + lax.ppermute(sent, "illum", pairs)
    return result


def solution(mesh):
    illums = mesh.shape["illum"]
    columns = 4 if illums % 4 == 0 else 1
    return jax.shard_map(
        functools.partial(on_device, columns=columns),
        mesh=mesh,
        in_specs=(
            P("depth", "illum", None, None, None),
            P("depth", None, None),
            P("depth", None, None),
            P("illum", None, None),
            P("illum"),
        ),
        out_specs=P("depth", None, "illum", None),
        check_vma=False,
    )
```

```python
import functools

import jax
import jax.numpy as jnp
import ml_dtypes
import numpy as np
from jax import lax
from jax.experimental import pallas as pl
from jax.experimental.pallas import tpu as pltpu
from jax.sharding import PartitionSpec as P

BF16 = jnp.bfloat16
F32 = jnp.float32
VMEM = pl.BlockSpec(memory_space=pltpu.VMEM)
SMEM = pl.BlockSpec(memory_space=pltpu.SMEM)
HBM = pl.BlockSpec(memory_space=pltpu.MemorySpace.HBM)


def operator_matrices(extent):
    counter = np.arange(extent)
    frequency = np.where(counter < extent // 2, counter, counter - extent)
    factor = np.exp(-2j * np.pi * ((frequency * frequency) % 1024) / 1024)
    table = np.exp(-2j * np.pi * ((counter[:, None] * counter[None, :]) % extent) / extent)
    operator = (np.conj(table) * factor[None, :]) @ table / extent
    operator = 0.5 * (operator + operator.T)
    terms = []
    for matrix in (operator.real, operator.imag - operator.real, operator.real + operator.imag):
        high = matrix.astype(np.float32).astype(ml_dtypes.bfloat16)
        low = (matrix - high.astype(np.float64)).astype(np.float32).astype(ml_dtypes.bfloat16)
        terms.append(np.stack([high, low]))
    return np.stack(terms)


def dot(left, right):
    return jnp.dot(left, right, preferred_element_type=F32)


def split(value):
    high = value.astype(BF16)
    return high, (value - high.astype(F32)).astype(BF16)


def from_right(value, matrices, which):
    high, low = split(value)
    w_high, w_low = matrices[which, 0], matrices[which, 1]
    return dot(
        jnp.concatenate([high, low, high], axis=1), jnp.concatenate([w_high, w_high, w_low], axis=0)
    )


def from_left(value, matrices, which):
    high, low = split(value)
    w_high, w_low = matrices[which, 0], matrices[which, 1]
    return dot(
        jnp.concatenate([w_high, w_high, w_low], axis=1), jnp.concatenate([high, low, high], axis=0)
    )


def adjoint(real, imag, matrices):
    both = from_right(real + imag, matrices, 0)
    mid_real = both + from_right(imag, matrices, 1)
    mid_imag = both - from_right(real, matrices, 2)
    both = from_left(mid_real + mid_imag, matrices, 0)
    return both + from_left(mid_imag, matrices, 1), both - from_left(mid_real, matrices, 2)


def entry_body(light, fields, s_real, s_imag, measured, table, x_ramp, y_ramp, out, psi, *refs):
    if light == 0:
        s_near, i_near, t_near, field, seen, sems = refs
    else:
        s_near, i_near, t_near = s_real, s_imag, table
        field, seen, sems = refs
    slabs = field.shape[0]
    last = slabs - 1
    copies = [pltpu.make_async_copy(fields.at[last, light], field.at[last], sems.at[0])]
    if light == 0:
        copies += [
            pltpu.make_async_copy(s_real, s_near, sems.at[1]),
            pltpu.make_async_copy(s_imag, i_near, sems.at[2]),
            pltpu.make_async_copy(table.at[0], t_near.at[0], sems.at[3]),
            pltpu.make_async_copy(table.at[1], t_near.at[1], sems.at[4]),
            pltpu.make_async_copy(table.at[2], t_near.at[2], sems.at[5]),
        ]
    later = [pltpu.make_async_copy(measured.at[light], seen, sems.at[6])]
    later += [
        pltpu.make_async_copy(fields.at[slab, light], field.at[slab], sems.at[7 + slab])
        for slab in range(last)
    ]
    for copy in copies + later:
        copy.start()
    c_x, d_x = x_ramp[0], x_ramp[1]
    c_y, d_y = y_ramp[0], y_ramp[1]
    cos, sin = c_x * c_y - d_x * d_y, d_x * c_y + c_x * d_y

    def tilt(slab):
        real, imag = field[slab, 0].astype(F32), field[slab, 1].astype(F32)
        psi[slab, 0] = cos * real - sin * imag
        psi[slab, 1] = cos * imag + sin * real

    for copy in copies:
        copy.wait()
    tilt(last)
    a_real, a_imag = s_near[last], i_near[last]
    f_real, f_imag = psi[last, 0], psi[last, 1]
    real, imag = adjoint(
        a_real * f_real - a_imag * f_imag, -(a_real * f_imag + a_imag * f_real), t_near
    )
    for copy in later:
        copy.wait()
    weight = 2.0 * (real * real + imag * imag - seen[...])
    out[0] = weight * real
    out[1] = -(weight * imag)
    for slab in range(last):
        tilt(slab)


def keep_body(flag, _, *refs):
    sources, targets, sems = refs[: len(refs) // 2], refs[len(refs) // 2 : -1], refs[-1]
    copies = [
        pltpu.make_async_copy(source, target, sems.at[index])
        for index, (source, target) in enumerate(zip(sources, targets))
    ]

    @pl.when(flag[0] > 0)
    def _():
        for copy in copies:
            copy.start()
        for copy in copies:
            copy.wait()


def section_body(scale, entries, chains, flag, *refs):
    chis, refs = refs[:entries], refs[entries:]
    s_real, s_imag, table, psi, *refs = refs
    if chains:
        low_real, low_imag, grad_in, out, middle, grad, fields, screens, sems = refs
    else:
        grad_in, out, grad, fields, sems = refs
    slabs = fields.shape[0]
    shape = (grad.shape[0], grad.shape[3], grad.shape[4])

    def field_copy(slab):
        return pltpu.make_async_copy(psi.at[slab], fields.at[slab], sems.at[slab])

    def low_copies(slab):
        return [
            pltpu.make_async_copy(low_real.at[slab], screens.at[0, slab], sems.at[slabs + slab]),
            pltpu.make_async_copy(low_imag.at[slab], screens.at[1, slab], sems.at[2 * slabs + slab]),
        ]

    @pl.when(flag[0] > 0)
    def _():
        for slab in reversed(range(slabs)):
            field_copy(slab).start()
        if chains:

            @pl.when(flag[0] == 1)
            def _():
                for slab in reversed(range(slabs)):
                    for copy in low_copies(slab):
                        copy.start()

        for index, chi in enumerate(chis):

            @pl.when(flag[0] == (index + 1 if entries > 1 or chains else flag[0]))
            def _(chi=chi):
                out[...] = chi[...]

        def step(index, carry):
            slab = slabs - 1 - index
            real, imag = adjoint(out[0], out[1], table)
            a_real, a_imag = s_real[slab], s_imag[slab]
            out[0] = a_real * real + a_imag * imag
            out[1] = a_real * imag - a_imag * real
            field_copy(slab).wait()
            p_real, p_imag = fields[slab, 0], fields[slab, 1]
            g_real = scale * (p_real * real + p_imag * imag)
            g_imag = scale * (p_real * imag - p_imag * real)
            grad[:, slab, 0] = grad_in[:, slab, 0] + g_real.reshape(shape)
            grad[:, slab, 1] = grad_in[:, slab, 1] + g_imag.reshape(shape)
            return carry

        lax.fori_loop(0, slabs, step, 0)
        if chains:
            middle[...] = out[...]

            @pl.when(flag[0] == 1)
            def _():
                def onward(index, carry):
                    slab = slabs - 1 - index
                    real, imag = adjoint(out[0], out[1], table)
                    for copy in low_copies(slab):
                        copy.wait()
                    a_real, a_imag = screens[0, slab], screens[1, slab]
                    out[0] = a_real * real + a_imag * imag
                    out[1] = a_real * imag - a_imag * real
                    return carry

                lax.fori_loop(0, slabs, onward, 0)

    @pl.when(flag[0] == 0)
    def _():
        grad[...] = grad_in[...]


def on_device(fields, screen_real, screen_imag, measured, angles, *, columns):
    slabs, lights, _, extent, _ = fields.shape
    segments = lax.axis_size("depth")
    position = lax.axis_index("depth")
    groups = lax.axis_size("illum")
    counter = jnp.arange(extent, dtype=jnp.int32)

    def ramp(shift):
        angle = 2.0 * jnp.pi / extent * ((shift[:, None] * counter) % extent).astype(F32)
        return jnp.stack([jnp.cos(angle), jnp.sin(angle)], axis=1)

    x_ramp = ramp(angles % 16 - 8)[..., None]
    y_ramp = ramp(angles // 16 - 8)[:, :, None, :]

    def far(value):
        return pltpu.with_memory_space_constraint(value, pltpu.MemorySpace.HBM)

    def like(value):
        return jax.ShapeDtypeStruct(value.shape, value.dtype)

    state_shape = jax.ShapeDtypeStruct((2, extent, extent), F32)
    psi_shape = jax.ShapeDtypeStruct((slabs, 2, extent, extent), F32)
    grad_shape = jax.ShapeDtypeStruct((groups, slabs, 2, extent // groups, extent), F32)
    work = 18 * 2 * extent**3
    params = pltpu.CompilerParams(vmem_limit_bytes=24 << 20)
    scale = float(lights * groups) ** -0.5

    def cost(count):
        return pl.CostEstimate(flops=count * work, bytes_accessed=1 << 20, transcendentals=0)

    def keep(flag, after, *values):
        return pl.pallas_call(
            keep_body,
            out_shape=[like(value) for value in values],
            in_specs=[SMEM] + [HBM] * (len(values) + 1),
            out_specs=[VMEM] * len(values),
            scratch_shapes=[pltpu.SemaphoreType.DMA((len(values),))],
            compiler_params=params,
            cost_estimate=cost(1),
            name="keep",
        )(flag, far(after), *map(far, values))

    def entry(light, s_real, s_imag, table):
        first = light == 0
        return pl.pallas_call(
            functools.partial(entry_body, light),
            out_shape=[state_shape, psi_shape]
            + ([like(s_real), like(s_imag), like(table)] if first else []),
            in_specs=[HBM] + ([HBM] if first else [VMEM]) * 2 + [HBM, HBM if first else VMEM, VMEM, VMEM],
            out_specs=[VMEM] * (5 if first else 2),
            scratch_shapes=[
                pltpu.VMEM((slabs, 2, extent, extent), BF16),
                pltpu.VMEM((extent, extent), F32),
                pltpu.SemaphoreType.DMA((7 + slabs,)),
            ],
            compiler_params=params,
            cost_estimate=cost(2),
            name="entry",
        )(far(fields), *((far(s_real), far(s_imag)) if first else (s_real, s_imag)), far(measured),
          far(table) if first else table, x_ramp[light], y_ramp[light])

    def section(flag, chis, s_real, s_imag, table, psi, low, grad):
        entries, chains = len(chis), low is not None
        outs = 2 if chains else 1
        aliased = 1 + entries + 4 + (2 if chains else 0)
        return pl.pallas_call(
            functools.partial(section_body, scale, entries, chains),
            out_shape=[state_shape] * outs + [grad_shape],
            in_specs=[SMEM] + [VMEM] * (entries + 3) + [HBM] * (3 if chains else 1) + [VMEM],
            out_specs=[VMEM] * (outs + 1),
            scratch_shapes=[pltpu.VMEM(psi_shape.shape, F32)]
            + ([pltpu.VMEM((2, slabs, extent, extent), F32)] if chains else [])
            + [pltpu.SemaphoreType.DMA((3 * slabs,))],
            input_output_aliases={aliased: outs},
            compiler_params=params,
            cost_estimate=cost(slabs * outs),
            name="section",
        )(flag, *chis, s_real, s_imag, table, far(psi), *([far(part) for part in low] if chains else []), grad)

    pairs = segments // 2
    swap = [(2 * c + 1, 2 * c) for c in range(pairs)] + [(2 * c, 2 * c + 1) for c in range(pairs)]
    down = [(2 * c + 1, 2 * ((c - 1) % pairs) + 1) for c in range(pairs)]
    low = [lax.ppermute(screen_real, "depth", swap), lax.ppermute(screen_imag, "depth", swap)]
    matrices = jnp.asarray(operator_matrices(extent))
    upper = position % 2 == 1
    stage_of = pairs - 1 - position // 2
    arrived, psis, near = [], [], [screen_real, screen_imag, matrices]
    for light in range(lights):
        chi, psi, *held = entry(light, *near)
        near = held or near
        arrived.append(chi)
        psis.append(psi)
    grad = jnp.zeros(grad_shape.shape, F32)
    middle = [None] * lights
    for stage in range(pairs + 1):
        first = jnp.logical_and(upper, stage_of == stage).astype(jnp.int32)[None]
        second = jnp.logical_and(jnp.logical_not(upper), stage_of == stage - 1)
        second = second.astype(jnp.int32)[None]
        flag = first + 2 * second if stage < pairs else second
        if stage > 0:
            near = keep(flag, before, screen_real, screen_imag, matrices)
        for light in range(lights):
            chis = [value for value in (arrived[light], middle[light]) if value is not None]
            left, *middles, grad = section(
                flag, chis, *near, psis[light], low if stage < pairs - 1 else None, grad
            )
            if light == 0:
                before = left
            arrived[light] = middle[light] = None
            if stage < pairs - 1:
                arrived[light] = lax.ppermute(left, "depth", down)
                middle[light] = lax.ppermute(middles[0], "depth", swap)
            elif stage < pairs:
                middle[light] = lax.ppermute(left, "depth", swap)
    return owned_sum(grad, groups, columns)


def owned_sum(value, groups, columns):
    pair = 2
    quarters = groups // (columns * pair)
    blocks = value.reshape(columns, quarters, pair, *value.shape[1:])
    here = lax.axis_index("illum")
    column, quarter, digit = here // (quarters * pair), here // pair % quarters, here % pair

    def index(c, q, d):
        return (c % columns * quarters + q % quarters) * pair + d % pair

    places = [(c, q, d) for c in range(columns) for q in range(quarters) for d in range(pair)]

    def block(c, d):
        part = lax.dynamic_index_in_dim(blocks, (column + c) % columns, 0, keepdims=False)
        return lax.dynamic_index_in_dim(part, (digit + d) % pair, 1, keepdims=False)

    total = block(0, 0)
    for d in range(pair):
        for c in range(columns):
            if (c, d) != (0, 0):
                route = [(index(*p), index(p[0] + c, p[1], p[2] + d)) for p in places]
                total = total + lax.ppermute(block(c, d), "illum", route)
    result = lax.dynamic_index_in_dim(total, quarter, 0, keepdims=False)
    for q in range(1, quarters):
        route = [(index(*p), index(p[0], p[1] + q, p[2])) for p in places]
        sent = lax.dynamic_index_in_dim(total, (quarter + q) % quarters, 0, keepdims=False)
        result = result + lax.ppermute(sent, "illum", route)
    return result


def solution(mesh):
    illums = mesh.shape["illum"]
    columns = 4 if illums % 8 == 0 else 1
    return jax.shard_map(
        functools.partial(on_device, columns=columns),
        mesh=mesh,
        in_specs=(
            P("depth", "illum", None, None, None),
            P("depth", None, None),
            P("depth", None, None),
            P("illum", None, None),
            P("illum"),
        ),
        out_specs=P("depth", None, "illum", None),
        check_vma=False,
    )
```

```python
import functools

import jax
import jax.numpy as jnp
import ml_dtypes
import numpy as np
from jax import lax
from jax.experimental import pallas as pl
from jax.experimental.pallas import tpu as pltpu
from jax.sharding import PartitionSpec as P

BF16 = jnp.bfloat16
F32 = jnp.float32
VMEM = pl.BlockSpec(memory_space=pltpu.VMEM)
SMEM = pl.BlockSpec(memory_space=pltpu.SMEM)
HBM = pl.BlockSpec(memory_space=pltpu.MemorySpace.HBM)


def operator_matrices(extent):
    counter = np.arange(extent)
    frequency = np.where(counter < extent // 2, counter, counter - extent)
    factor = np.exp(-2j * np.pi * ((frequency * frequency) % 1024) / 1024)
    table = np.exp(-2j * np.pi * ((counter[:, None] * counter[None, :]) % extent) / extent)
    operator = (np.conj(table) * factor[None, :]) @ table / extent
    operator = 0.5 * (operator + operator.T)
    terms = []
    for matrix in (operator.real, operator.imag - operator.real, operator.real + operator.imag):
        high = matrix.astype(np.float32).astype(ml_dtypes.bfloat16)
        low = (matrix - high.astype(np.float64)).astype(np.float32).astype(ml_dtypes.bfloat16)
        terms.append(np.stack([high, low]))
    return np.stack(terms)


def dot(left, right):
    return jnp.dot(left, right, preferred_element_type=F32)


def split(value):
    high = value.astype(BF16)
    return high, (value - high.astype(F32)).astype(BF16)


def from_right(value, matrices, which):
    high, low = split(value)
    w_high, w_low = matrices[which, 0], matrices[which, 1]
    return dot(
        jnp.concatenate([high, low, high], axis=1), jnp.concatenate([w_high, w_high, w_low], axis=0)
    )


def from_left(value, matrices, which):
    high, low = split(value)
    w_high, w_low = matrices[which, 0], matrices[which, 1]
    return dot(
        jnp.concatenate([w_high, w_high, w_low], axis=1), jnp.concatenate([high, low, high], axis=0)
    )


def adjoint(real, imag, matrices):
    both = from_right(real + imag, matrices, 0)
    mid_real = both + from_right(imag, matrices, 1)
    mid_imag = both - from_right(real, matrices, 2)
    both = from_left(mid_real + mid_imag, matrices, 0)
    return both + from_left(mid_imag, matrices, 1), both - from_left(mid_real, matrices, 2)


def entry_body(light, fields, s_real, s_imag, measured, table, x_ramp, y_ramp, out, psi_out,
               s_near, i_near, t_near, field, seen, psi, sems):
    slabs = field.shape[0]
    last = slabs - 1
    copies = [
        pltpu.make_async_copy(fields.at[last, light], field.at[last], sems.at[0]),
        pltpu.make_async_copy(s_real, s_near, sems.at[1]),
        pltpu.make_async_copy(s_imag, i_near, sems.at[2]),
        pltpu.make_async_copy(table.at[0], t_near.at[0], sems.at[3]),
        pltpu.make_async_copy(table.at[1], t_near.at[1], sems.at[4]),
        pltpu.make_async_copy(table.at[2], t_near.at[2], sems.at[5]),
    ]
    later = [pltpu.make_async_copy(measured.at[light], seen, sems.at[6])]
    later += [
        pltpu.make_async_copy(fields.at[slab, light], field.at[slab], sems.at[7 + slab])
        for slab in range(last)
    ]
    stores = [
        pltpu.make_async_copy(psi.at[slab], psi_out.at[slab], sems.at[7 + slabs + slab])
        for slab in range(slabs)
    ]
    for copy in copies + later:
        copy.start()
    c_x, d_x = x_ramp[0], x_ramp[1]
    c_y, d_y = y_ramp[0], y_ramp[1]
    cos, sin = c_x * c_y - d_x * d_y, d_x * c_y + c_x * d_y

    def tilt(slab):
        real, imag = field[slab, 0].astype(F32), field[slab, 1].astype(F32)
        psi[slab, 0] = cos * real - sin * imag
        psi[slab, 1] = cos * imag + sin * real

    for copy in copies:
        copy.wait()
    tilt(last)
    stores[last].start()
    a_real, a_imag = s_near[last], i_near[last]
    f_real, f_imag = psi[last, 0], psi[last, 1]
    for copy in later:
        copy.wait()
    for slab in range(last):
        tilt(slab)
        stores[slab].start()
    real, imag = adjoint(
        a_real * f_real - a_imag * f_imag, -(a_real * f_imag + a_imag * f_real), t_near
    )
    weight = 2.0 * (real * real + imag * imag - seen[...])
    out[0] = weight * real
    out[1] = -(weight * imag)
    for store in stores:
        store.wait()


def keep_body(flag, _, *refs):
    sources, targets, sems = refs[: len(refs) // 2], refs[len(refs) // 2 : -1], refs[-1]
    copies = [
        pltpu.make_async_copy(source, target, sems.at[index])
        for index, (source, target) in enumerate(zip(sources, targets))
    ]

    @pl.when(flag[0] > 0)
    def _():
        for copy in copies:
            copy.start()
        for copy in copies:
            copy.wait()


def section_body(scale, kinds, flag, *refs):
    arrives, comes, chains, leaves, near = kinds
    refs = list(refs)
    sems = refs.pop()
    chi = refs.pop(0) if arrives else None
    partner = refs.pop(0) if comes else None
    s_real, s_imag, table, psi = refs[:4]
    del refs[:4]
    if chains:
        low_real, low_imag = refs[:2]
        del refs[:2]
    grad_in = refs.pop(0)
    middle_out = refs.pop(0) if chains else None
    if leaves:
        out, grad = refs[:2]
        del refs[:2]
    else:
        grad, out = refs[:2]
        del refs[:2]
    middle = refs.pop(0) if chains else None
    if not near:
        fields = refs.pop(0)
    screens = refs.pop(0) if chains else None
    slabs = psi.shape[0]
    rows = grad.shape[3]

    def field_copy(slab):
        return pltpu.make_async_copy(psi.at[slab], fields.at[slab], sems.at[slab])

    def low_copies(slab):
        return [
            pltpu.make_async_copy(low_real.at[slab], screens.at[0, slab], sems.at[slabs + slab]),
            pltpu.make_async_copy(low_imag.at[slab], screens.at[1, slab], sems.at[2 * slabs + slab]),
        ]

    def add(slab, part, value):
        blocks = value.reshape(grad.shape[0], rows, value.shape[1])
        grad[:, slab, part] = grad_in[:, slab, part] + blocks

    @pl.when(flag[0] > 0)
    def _():
        if not near:
            for slab in reversed(range(slabs)):
                field_copy(slab).start()
        if chains:

            @pl.when(flag[0] == 1)
            def _():
                for slab in reversed(range(slabs)):
                    for copy in low_copies(slab):
                        copy.start()

        if arrives and comes:

            @pl.when(flag[0] == 1)
            def _():
                out[...] = chi[...]

            @pl.when(flag[0] == 2)
            def _():
                fetch = pltpu.make_async_copy(partner, out, sems.at[3 * slabs])
                fetch.start()
                fetch.wait()
        else:
            out[...] = chi[...] if arrives else partner[...]

        def step(index, carry):
            slab = slabs - 1 - index
            real, imag = adjoint(out[0], out[1], table)
            a_real, a_imag = s_real[slab], s_imag[slab]
            out[0] = a_real * real + a_imag * imag
            out[1] = a_real * imag - a_imag * real
            if near:
                p_real, p_imag = psi[slab, 0], psi[slab, 1]
            else:
                field_copy(slab).wait()
                p_real, p_imag = fields[slab, 0], fields[slab, 1]
            add(slab, 0, scale * (p_real * real + p_imag * imag))
            add(slab, 1, scale * (p_real * imag - p_imag * real))
            return carry

        lax.fori_loop(0, slabs, step, 0)
        if chains:

            @pl.when(flag[0] == 1)
            def _():
                middle[...] = out[...]
                store = pltpu.make_async_copy(middle, middle_out, sems.at[3 * slabs + 1])
                store.start()

                def onward(index, carry):
                    slab = slabs - 1 - index
                    real, imag = adjoint(out[0], out[1], table)
                    for copy in low_copies(slab):
                        copy.wait()
                    a_real, a_imag = screens[0, slab], screens[1, slab]
                    out[0] = a_real * real + a_imag * imag
                    out[1] = a_real * imag - a_imag * real
                    return carry

                lax.fori_loop(0, slabs, onward, 0)
                store.wait()

    @pl.when(flag[0] == 0)
    def _():
        grad[...] = grad_in[...]


def on_device(fields, screen_real, screen_imag, measured, angles, *, columns):
    slabs, lights, _, extent, _ = fields.shape
    segments = lax.axis_size("depth")
    position = lax.axis_index("depth")
    groups = lax.axis_size("illum")
    counter = jnp.arange(extent, dtype=jnp.int32)

    def ramp(shift):
        angle = 2.0 * jnp.pi / extent * ((shift[:, None] * counter) % extent).astype(F32)
        return jnp.stack([jnp.cos(angle), jnp.sin(angle)], axis=1)

    x_ramp = ramp(angles % 16 - 8)[..., None]
    y_ramp = ramp(angles // 16 - 8)[:, :, None, :]

    def far(value):
        return pltpu.with_memory_space_constraint(value, pltpu.MemorySpace.HBM)

    def like(value):
        return jax.ShapeDtypeStruct(value.shape, value.dtype)

    state_shape = jax.ShapeDtypeStruct((2, extent, extent), F32)
    psi_shape = jax.ShapeDtypeStruct((slabs, 2, extent, extent), F32)
    grad_shape = jax.ShapeDtypeStruct((groups, slabs, 2, extent // groups, extent), F32)
    work = 18 * 2 * extent**3
    params = pltpu.CompilerParams(vmem_limit_bytes=24 << 20)
    scale = float(lights * groups) ** -0.5

    def cost(count):
        return pl.CostEstimate(flops=count * work, bytes_accessed=1 << 20, transcendentals=0)

    def keep(flag, after, *values):
        return pl.pallas_call(
            keep_body,
            out_shape=[like(value) for value in values],
            in_specs=[SMEM] + [HBM] * (len(values) + 1),
            out_specs=[VMEM] * len(values),
            scratch_shapes=[pltpu.SemaphoreType.DMA((len(values),))],
            compiler_params=params,
            cost_estimate=cost(1),
            name="keep",
        )(flag, far(after), *map(far, values))

    def entry(light):
        return pl.pallas_call(
            functools.partial(entry_body, light),
            out_shape=[state_shape, pltpu.MemorySpace.HBM(psi_shape.shape, F32)]
            + [like(value) for value in (screen_real, screen_imag, matrices)],
            in_specs=[HBM] * 5 + [VMEM] * 2,
            out_specs=[VMEM, HBM] + [VMEM] * 3,
            scratch_shapes=[
                pltpu.VMEM((slabs, 2, extent, extent), BF16),
                pltpu.VMEM((extent, extent), F32),
                pltpu.VMEM(psi_shape.shape, F32),
                pltpu.SemaphoreType.DMA((7 + 2 * slabs,)),
            ],
            compiler_params=params,
            cost_estimate=cost(2),
            name="entry",
        )(*map(far, (fields, screen_real, screen_imag, measured, matrices)), x_ramp[light], y_ramp[light])

    def section(flag, chi, partner, s_real, s_imag, table, psi, low, grad, leaves, near):
        arrives, comes, chains = chi is not None, partner is not None, low is not None
        where, place = (VMEM, lambda value: value) if near else (HBM, far)
        operands = [(SMEM, flag)]
        if arrives:
            operands.append((VMEM, chi))
        if comes:
            operands.append((HBM, far(partner)) if arrives else (VMEM, partner))
        operands += [(VMEM, s_real), (VMEM, s_imag), (VMEM, table), (where, place(psi))]
        if chains:
            operands += [(HBM, far(part)) for part in low]
        operands.append((VMEM, grad))
        results, scratch = [(VMEM, grad_shape)], []
        if leaves:
            results.insert(0, (VMEM, state_shape))
        else:
            scratch.append(pltpu.VMEM(state_shape.shape, F32))
        if chains:
            results.insert(0, (HBM, pltpu.MemorySpace.HBM(state_shape.shape, F32)))
            scratch.append(pltpu.VMEM(state_shape.shape, F32))
        if not near:
            scratch.append(pltpu.VMEM(psi_shape.shape, F32))
        if chains:
            scratch.append(pltpu.VMEM((2, slabs, extent, extent), F32))
        scratch.append(pltpu.SemaphoreType.DMA((3 * slabs + 2,)))
        kinds = (arrives, comes, chains, leaves, near)
        return pl.pallas_call(
            functools.partial(section_body, scale, kinds),
            out_shape=[shape for _, shape in results],
            in_specs=[spec for spec, _ in operands],
            out_specs=[spec for spec, _ in results],
            scratch_shapes=scratch,
            input_output_aliases={len(operands) - 1: len(results) - 1},
            compiler_params=params,
            cost_estimate=cost(slabs * (2 if chains else 1)),
            name="section",
        )(*[value for _, value in operands])

    pairs = segments // 2
    swap = [(2 * c + 1, 2 * c) for c in range(pairs)] + [(2 * c, 2 * c + 1) for c in range(pairs)]
    low = [lax.ppermute(screen_real, "depth", swap), lax.ppermute(screen_imag, "depth", swap)]
    matrices = jnp.asarray(operator_matrices(extent))
    upper = position % 2 == 1
    stage_of = pairs - 1 - position // 2
    grad = jnp.zeros(grad_shape.shape, F32)
    arrived, middle, psis = [None] * lights, [None] * lights, [None] * lights

    def taken(stage):
        first = jnp.logical_and(upper, stage_of == stage).astype(jnp.int32)[None]
        second = jnp.logical_and(jnp.logical_not(upper), stage_of == stage - 1)
        return first, second.astype(jnp.int32)[None]

    for stage in range(pairs - 1):
        here = pairs - 1 - stage
        first, second = taken(stage)
        flag = first + 2 * second
        for light in range(lights):
            if stage == 0:
                arrived[light], psis[light], *near = entry(light)
            else:
                near = keep(flag, before, screen_real, screen_imag, matrices)
            middle_now, before, grad = section(
                flag, arrived[light], middle[light], *near, psis[light], low, grad, True, False
            )
            arrived[light] = lax.ppermute(before, "depth", [(2 * here + 1, 2 * here - 1)])
            middle[light] = lax.ppermute(
                middle_now, "depth", [(2 * here + 1, 2 * here), (2 * here, 2 * here + 1)]
            )
    first, second = taken(pairs - 1)
    flag = first + 2 * second
    lefts = []
    for light in range(lights):
        near = keep(flag, before, screen_real, screen_imag, matrices)
        left, grad = section(
            flag, arrived[light], middle[light], *near, psis[light], None, grad, True, False
        )
        before = left
        lefts.append(left)
    _, last = taken(pairs)
    for light in range(lights):
        near = keep(last, lefts[light], screen_real, screen_imag, matrices)
        if light > 0:
            lefts[light], grad = lax.optimization_barrier((lefts[light], grad))
        handed = lax.ppermute(lefts[light], "depth", [(1, 0)])
        (grad,) = section(last, None, handed, *near, psis[light], None, grad, False, False)
    return owned_sum(grad, groups, columns)


def owned_sum(value, groups, columns):
    pair = 2
    quarters = groups // (columns * pair)
    blocks = value.reshape(columns, quarters, pair, *value.shape[1:])
    here = lax.axis_index("illum")
    column, quarter, digit = here // (quarters * pair), here // pair % quarters, here % pair

    def index(c, q, d):
        return (c % columns * quarters + q % quarters) * pair + d % pair

    places = [(c, q, d) for c in range(columns) for q in range(quarters) for d in range(pair)]

    def block(c, d):
        part = lax.dynamic_index_in_dim(blocks, (column + c) % columns, 0, keepdims=False)
        return lax.dynamic_index_in_dim(part, (digit + d) % pair, 1, keepdims=False)

    total = block(0, 0)
    for d in range(pair):
        for c in range(columns):
            if (c, d) != (0, 0):
                route = [(index(*p), index(p[0] + c, p[1], p[2] + d)) for p in places]
                total = total + lax.ppermute(block(c, d), "illum", route)
    result = lax.dynamic_index_in_dim(total, quarter, 0, keepdims=False)
    for q in range(1, quarters):
        route = [(index(*p), index(p[0], p[1] + q, p[2])) for p in places]
        sent = lax.dynamic_index_in_dim(total, (quarter + q) % quarters, 0, keepdims=False)
        result = result + lax.ppermute(sent, "illum", route)
    return result


def solution(mesh):
    illums = mesh.shape["illum"]
    columns = 4 if illums % 8 == 0 else 1
    return jax.shard_map(
        functools.partial(on_device, columns=columns),
        mesh=mesh,
        in_specs=(
            P("depth", "illum", None, None, None),
            P("depth", None, None),
            P("depth", None, None),
            P("illum", None, None),
            P("illum"),
        ),
        out_specs=P("depth", None, "illum", None),
        check_vma=False,
    )
```

```python
import functools

import jax
import jax.numpy as jnp
import ml_dtypes
import numpy as np
from jax import lax
from jax.experimental import pallas as pl
from jax.experimental.pallas import tpu as pltpu
from jax.sharding import PartitionSpec as P

BF16 = jnp.bfloat16
F32 = jnp.float32
VMEM = pl.BlockSpec(memory_space=pltpu.VMEM)
SMEM = pl.BlockSpec(memory_space=pltpu.SMEM)
HBM = pl.BlockSpec(memory_space=pltpu.MemorySpace.HBM)


def operator_matrices(extent):
    counter = np.arange(extent)
    frequency = np.where(counter < extent // 2, counter, counter - extent)
    factor = np.exp(-2j * np.pi * ((frequency * frequency) % 1024) / 1024)
    table = np.exp(-2j * np.pi * ((counter[:, None] * counter[None, :]) % extent) / extent)
    operator = (np.conj(table) * factor[None, :]) @ table / extent
    operator = 0.5 * (operator + operator.T)
    terms = []
    for matrix in (operator.real, operator.imag - operator.real, operator.real + operator.imag):
        high = matrix.astype(np.float32).astype(ml_dtypes.bfloat16)
        low = (matrix - high.astype(np.float64)).astype(np.float32).astype(ml_dtypes.bfloat16)
        terms.append(np.stack([high, low]))
    return np.stack(terms)


def dot(left, right):
    return jnp.dot(left, right, preferred_element_type=F32)


def split(value):
    high = value.astype(BF16)
    return high, (value - high.astype(F32)).astype(BF16)


def from_right(value, matrices, which):
    high, low = split(value)
    w_high, w_low = matrices[which, 0], matrices[which, 1]
    return dot(
        jnp.concatenate([high, low, high], axis=1), jnp.concatenate([w_high, w_high, w_low], axis=0)
    )


def from_left(value, matrices, which):
    high, low = split(value)
    w_high, w_low = matrices[which, 0], matrices[which, 1]
    return dot(
        jnp.concatenate([w_high, w_high, w_low], axis=1), jnp.concatenate([high, low, high], axis=0)
    )


def adjoint(real, imag, matrices):
    both = from_right(real + imag, matrices, 0)
    mid_real = both + from_right(imag, matrices, 1)
    mid_imag = both - from_right(real, matrices, 2)
    both = from_left(mid_real + mid_imag, matrices, 0)
    return both + from_left(mid_imag, matrices, 1), both - from_left(mid_real, matrices, 2)


def entry_body(light, fields, s_real, s_imag, measured, table, x_ramp, y_ramp, out, psi_out,
               s_near, i_near, t_near, field, seen, psi, sems):
    slabs = field.shape[0]
    last = slabs - 1
    copies = [
        pltpu.make_async_copy(fields.at[last, light], field.at[last], sems.at[0]),
        pltpu.make_async_copy(s_real.at[last], s_near.at[last], sems.at[1]),
        pltpu.make_async_copy(s_imag.at[last], i_near.at[last], sems.at[2]),
        pltpu.make_async_copy(table.at[0], t_near.at[0], sems.at[3]),
        pltpu.make_async_copy(table.at[1], t_near.at[1], sems.at[4]),
        pltpu.make_async_copy(table.at[2], t_near.at[2], sems.at[5]),
    ]
    later = [pltpu.make_async_copy(measured.at[light], seen, sems.at[6])]
    later += [
        pltpu.make_async_copy(fields.at[slab, light], field.at[slab], sems.at[7 + slab])
        for slab in range(last)
    ]
    stores = [
        pltpu.make_async_copy(psi.at[slab], psi_out.at[slab], sems.at[7 + slabs + slab])
        for slab in range(slabs)
    ]
    rest = [
        pltpu.make_async_copy(source.at[slab], target.at[slab], sems.at[7 + 2 * slabs + 2 * slab + part])
        for slab in range(last)
        for part, (source, target) in enumerate(((s_real, s_near), (s_imag, i_near)))
    ]
    for copy in copies + later + rest:
        copy.start()
    c_x, d_x = x_ramp[0], x_ramp[1]
    c_y, d_y = y_ramp[0], y_ramp[1]
    cos, sin = c_x * c_y - d_x * d_y, d_x * c_y + c_x * d_y

    def tilt(slab):
        real, imag = field[slab, 0].astype(F32), field[slab, 1].astype(F32)
        psi[slab, 0] = cos * real - sin * imag
        psi[slab, 1] = cos * imag + sin * real

    for copy in copies:
        copy.wait()
    tilt(last)
    stores[last].start()
    a_real, a_imag = s_near[last], i_near[last]
    f_real, f_imag = psi[last, 0], psi[last, 1]
    for copy in later:
        copy.wait()
    for slab in range(last):
        tilt(slab)
        stores[slab].start()
    real, imag = adjoint(
        a_real * f_real - a_imag * f_imag, -(a_real * f_imag + a_imag * f_real), t_near
    )
    weight = 2.0 * (real * real + imag * imag - seen[...])
    out[0] = weight * real
    out[1] = -(weight * imag)
    for copy in rest + stores:
        copy.wait()


def keep_body(flag, _, *refs):
    sources, targets, sems = refs[: len(refs) // 2], refs[len(refs) // 2 : -1], refs[-1]
    copies = [
        pltpu.make_async_copy(source, target, sems.at[index])
        for index, (source, target) in enumerate(zip(sources, targets))
    ]

    @pl.when(flag[0] > 0)
    def _():
        for copy in copies:
            copy.start()
        for copy in copies:
            copy.wait()


def section_body(scale, kinds, flag, *refs):
    arrives, comes, chains, leaves, near = kinds
    refs = list(refs)
    sems = refs.pop()
    chi = refs.pop(0) if arrives else None
    partner = refs.pop(0) if comes else None
    s_real, s_imag, table, psi = refs[:4]
    del refs[:4]
    if chains:
        low_real, low_imag = refs[:2]
        del refs[:2]
    grad_in = refs.pop(0)
    middle_out = refs.pop(0) if chains else None
    if leaves:
        out, grad = refs[:2]
        del refs[:2]
    else:
        grad, out = refs[:2]
        del refs[:2]
    middle = refs.pop(0) if chains else None
    if not near:
        fields = refs.pop(0)
    screens = refs.pop(0) if chains else None
    slabs = psi.shape[0]
    rows = grad.shape[3]

    def field_copy(slab):
        return pltpu.make_async_copy(psi.at[slab], fields.at[slab], sems.at[slab])

    def low_copies(slab):
        return [
            pltpu.make_async_copy(low_real.at[slab], screens.at[0, slab], sems.at[slabs + slab]),
            pltpu.make_async_copy(low_imag.at[slab], screens.at[1, slab], sems.at[2 * slabs + slab]),
        ]

    def add(slab, part, value):
        blocks = value.reshape(grad.shape[0], rows, value.shape[1])
        grad[:, slab, part] = grad_in[:, slab, part] + blocks

    @pl.when(flag[0] > 0)
    def _():
        if not near:
            for slab in reversed(range(slabs)):
                field_copy(slab).start()
        if chains:

            @pl.when(flag[0] == 1)
            def _():
                for slab in reversed(range(slabs)):
                    for copy in low_copies(slab):
                        copy.start()

        if arrives and comes:

            @pl.when(flag[0] == 1)
            def _():
                out[...] = chi[...]

            @pl.when(flag[0] == 2)
            def _():
                fetch = pltpu.make_async_copy(partner, out, sems.at[3 * slabs])
                fetch.start()
                fetch.wait()
        else:
            out[...] = chi[...] if arrives else partner[...]

        def step(index, carry):
            slab = slabs - 1 - index
            real, imag = adjoint(out[0], out[1], table)
            a_real, a_imag = s_real[slab], s_imag[slab]
            out[0] = a_real * real + a_imag * imag
            out[1] = a_real * imag - a_imag * real
            if near:
                p_real, p_imag = psi[slab, 0], psi[slab, 1]
            else:
                field_copy(slab).wait()
                p_real, p_imag = fields[slab, 0], fields[slab, 1]
            add(slab, 0, scale * (p_real * real + p_imag * imag))
            add(slab, 1, scale * (p_real * imag - p_imag * real))
            return carry

        lax.fori_loop(0, slabs, step, 0)
        if chains:

            @pl.when(flag[0] == 1)
            def _():
                middle[...] = out[...]
                store = pltpu.make_async_copy(middle, middle_out, sems.at[3 * slabs + 1])
                store.start()

                def onward(index, carry):
                    slab = slabs - 1 - index
                    real, imag = adjoint(out[0], out[1], table)
                    for copy in low_copies(slab):
                        copy.wait()
                    a_real, a_imag = screens[0, slab], screens[1, slab]
                    out[0] = a_real * real + a_imag * imag
                    out[1] = a_real * imag - a_imag * real
                    return carry

                lax.fori_loop(0, slabs, onward, 0)
                store.wait()

    @pl.when(flag[0] == 0)
    def _():
        grad[...] = grad_in[...]


def on_device(fields, screen_real, screen_imag, measured, angles, *, columns):
    slabs, lights, _, extent, _ = fields.shape
    segments = lax.axis_size("depth")
    position = lax.axis_index("depth")
    groups = lax.axis_size("illum")
    counter = jnp.arange(extent, dtype=jnp.int32)

    def ramp(shift):
        angle = 2.0 * jnp.pi / extent * ((shift[:, None] * counter) % extent).astype(F32)
        return jnp.stack([jnp.cos(angle), jnp.sin(angle)], axis=1)

    x_ramp = ramp(angles % 16 - 8)[..., None]
    y_ramp = ramp(angles // 16 - 8)[:, :, None, :]

    def far(value):
        return pltpu.with_memory_space_constraint(value, pltpu.MemorySpace.HBM)

    def like(value):
        return jax.ShapeDtypeStruct(value.shape, value.dtype)

    state_shape = jax.ShapeDtypeStruct((2, extent, extent), F32)
    psi_shape = jax.ShapeDtypeStruct((slabs, 2, extent, extent), F32)
    grad_shape = jax.ShapeDtypeStruct((groups, slabs, 2, extent // groups, extent), F32)
    work = 18 * 2 * extent**3
    params = pltpu.CompilerParams(vmem_limit_bytes=24 << 20)
    scale = float(lights * groups) ** -0.5

    def cost(count):
        return pl.CostEstimate(flops=count * work, bytes_accessed=1 << 20, transcendentals=0)

    def keep(flag, after, *values):
        return pl.pallas_call(
            keep_body,
            out_shape=[like(value) for value in values],
            in_specs=[SMEM] + [HBM] * (len(values) + 1),
            out_specs=[VMEM] * len(values),
            scratch_shapes=[pltpu.SemaphoreType.DMA((len(values),))],
            compiler_params=params,
            cost_estimate=cost(1),
            name="keep",
        )(flag, far(after), *map(far, values))

    def entry(light):
        return pl.pallas_call(
            functools.partial(entry_body, light),
            out_shape=[state_shape, pltpu.MemorySpace.HBM(psi_shape.shape, F32)]
            + [like(value) for value in (screen_real, screen_imag, matrices)],
            in_specs=[HBM] * 5 + [VMEM] * 2,
            out_specs=[VMEM, HBM] + [VMEM] * 3,
            scratch_shapes=[
                pltpu.VMEM((slabs, 2, extent, extent), BF16),
                pltpu.VMEM((extent, extent), F32),
                pltpu.VMEM(psi_shape.shape, F32),
                pltpu.SemaphoreType.DMA((7 + 4 * slabs,)),
            ],
            compiler_params=params,
            cost_estimate=cost(2),
            name="entry",
        )(*map(far, (fields, screen_real, screen_imag, measured, matrices)), x_ramp[light], y_ramp[light])

    def section(flag, chi, partner, s_real, s_imag, table, psi, low, grad, leaves, near):
        arrives, comes, chains = chi is not None, partner is not None, low is not None
        where, place = (VMEM, lambda value: value) if near else (HBM, far)
        operands = [(SMEM, flag)]
        if arrives:
            operands.append((VMEM, chi))
        if comes:
            operands.append((HBM, far(partner)) if arrives else (VMEM, partner))
        operands += [(VMEM, s_real), (VMEM, s_imag), (VMEM, table), (where, place(psi))]
        if chains:
            operands += [(HBM, far(part)) for part in low]
        operands.append((VMEM, grad))
        results, scratch = [(VMEM, grad_shape)], []
        if leaves:
            results.insert(0, (VMEM, state_shape))
        else:
            scratch.append(pltpu.VMEM(state_shape.shape, F32))
        if chains:
            results.insert(0, (HBM, pltpu.MemorySpace.HBM(state_shape.shape, F32)))
            scratch.append(pltpu.VMEM(state_shape.shape, F32))
        if not near:
            scratch.append(pltpu.VMEM(psi_shape.shape, F32))
        if chains:
            scratch.append(pltpu.VMEM((2, slabs, extent, extent), F32))
        scratch.append(pltpu.SemaphoreType.DMA((3 * slabs + 2,)))
        kinds = (arrives, comes, chains, leaves, near)
        return pl.pallas_call(
            functools.partial(section_body, scale, kinds),
            out_shape=[shape for _, shape in results],
            in_specs=[spec for spec, _ in operands],
            out_specs=[spec for spec, _ in results],
            scratch_shapes=scratch,
            input_output_aliases={len(operands) - 1: len(results) - 1},
            compiler_params=params,
            cost_estimate=cost(slabs * (2 if chains else 1)),
            name="section",
        )(*[value for _, value in operands])

    pairs = segments // 2
    swap = [(2 * c + 1, 2 * c) for c in range(pairs)] + [(2 * c, 2 * c + 1) for c in range(pairs)]
    low = [lax.ppermute(screen_real, "depth", swap), lax.ppermute(screen_imag, "depth", swap)]
    matrices = jnp.asarray(operator_matrices(extent))
    upper = position % 2 == 1
    stage_of = pairs - 1 - position // 2
    grad = jnp.zeros(grad_shape.shape, F32)
    arrived, middle, psis = [None] * lights, [None] * lights, [None] * lights

    def taken(stage):
        first = jnp.logical_and(upper, stage_of == stage).astype(jnp.int32)[None]
        second = jnp.logical_and(jnp.logical_not(upper), stage_of == stage - 1)
        return first, second.astype(jnp.int32)[None]

    for stage in range(pairs - 1):
        here = pairs - 1 - stage
        first, second = taken(stage)
        flag = first + 2 * second
        for light in range(lights):
            if stage == 0:
                arrived[light], psis[light], *near = entry(light)
            else:
                near = keep(flag, before, screen_real, screen_imag, matrices)
            middle_now, before, grad = section(
                flag, arrived[light], middle[light], *near, psis[light], low, grad, True, False
            )
            arrived[light] = lax.ppermute(before, "depth", [(2 * here + 1, 2 * here - 1)])
            middle[light] = lax.ppermute(
                middle_now, "depth", [(2 * here + 1, 2 * here), (2 * here, 2 * here + 1)]
            )
    first, second = taken(pairs - 1)
    flag = first + 2 * second
    lefts = []
    for light in range(lights):
        near = keep(flag, before, screen_real, screen_imag, matrices)
        left, grad = section(
            flag, arrived[light], middle[light], *near, psis[light], None, grad, True, False
        )
        before = left
        lefts.append(left)
    _, last = taken(pairs)
    for light in range(lights):
        near = keep(last, lefts[light], screen_real, screen_imag, matrices)
        if light > 0:
            lefts[light], grad = lax.optimization_barrier((lefts[light], grad))
        handed = lax.ppermute(lefts[light], "depth", [(1, 0)])
        (grad,) = section(last, None, handed, *near, psis[light], None, grad, False, False)
    return owned_sum(grad, groups, columns)


def owned_sum(value, groups, columns):
    pair = 2
    quarters = groups // (columns * pair)
    blocks = value.reshape(columns, quarters, pair, *value.shape[1:])
    here = lax.axis_index("illum")
    column, quarter, digit = here // (quarters * pair), here // pair % quarters, here % pair

    def index(c, q, d):
        return (c % columns * quarters + q % quarters) * pair + d % pair

    places = [(c, q, d) for c in range(columns) for q in range(quarters) for d in range(pair)]

    def block(c, d):
        part = lax.dynamic_index_in_dim(blocks, (column + c) % columns, 0, keepdims=False)
        return lax.dynamic_index_in_dim(part, (digit + d) % pair, 1, keepdims=False)

    total = block(0, 0)
    for d in range(pair):
        for c in range(columns):
            if (c, d) != (0, 0):
                route = [(index(*p), index(p[0] + c, p[1], p[2] + d)) for p in places]
                total = total + lax.ppermute(block(c, d), "illum", route)
    result = lax.dynamic_index_in_dim(total, quarter, 0, keepdims=False)
    for q in range(1, quarters):
        route = [(index(*p), index(p[0], p[1] + q, p[2])) for p in places]
        sent = lax.dynamic_index_in_dim(total, (quarter + q) % quarters, 0, keepdims=False)
        result = result + lax.ppermute(sent, "illum", route)
    return result


def solution(mesh):
    illums = mesh.shape["illum"]
    columns = 4 if illums % 8 == 0 else 1
    return jax.shard_map(
        functools.partial(on_device, columns=columns),
        mesh=mesh,
        in_specs=(
            P("depth", "illum", None, None, None),
            P("depth", None, None),
            P("depth", None, None),
            P("illum", None, None),
            P("illum"),
        ),
        out_specs=P("depth", None, "illum", None),
        check_vma=False,
    )
```
